512 devices in a mesh: section: 8 (over x, z_hi), ctx: 32 (over z_lo, y), tp: 2 (over core).
Axes of the slice: x: 4, y: 4, z: 16 (z_hi: 2, z_lo: 8; z = z_hi * 8 + z_lo), core: 2. Of those that a mesh axis runs over, the one named last changes fastest.
Arguments:
- queries: bfloat16 [8, 2, 4096, 4096], P('section', None, 'ctx', 'tp'), may hold values from -48 to 48
- keyvals: bfloat16 [8, 2, 2, 4096, 512], P('section', None, None, ('ctx', 'tp')), may hold values from -4 to 4
- segments: int32 [8, 2, 4096], P('section', None, 'ctx'), may hold values from 0 to 3, never falling along the last dimension, each value on 1 to 3072 neighbouring positions
Outputs:
- handed: bfloat16 [8, 2, 4096, 4096], P('section', None, 'ctx', 'tp')
The draws below stay inside these ranges and needn't reach their ends.
Inputs may be any that keep to these rules, and one draw needn't show every extreme that they name: `segments`: document numbers never fall along a stream; each document is at most 3072 positions long, and one is exactly that long.
All inputs are finite; a program needn't handle non-finite values.
Results may differ from the reference program's by a relative error of at most 0.0035.
Values may be sent and summed in bfloat16 or wider, within the bound.
No kernel may reach another device: no remote copies, remote signals or barrier semaphores. Data moves between devices by JAX's collectives and lax.ppermute only.
A program may use at most 128 MiB of HBM per device.

```python
import math
import jax
import jax.numpy as jnp
import numpy as np
from jax import lax

HEADS = 32
KVH = 4
HD = 128
SEQ = 4096
SECTIONS = 8


def shared_keys(key):
    shape = (SECTIONS, 2, SEQ, KVH, HD)
    key_rows = jnp.clip(jax.random.normal(jax.random.fold_in(key, 11), shape, jnp.float32), -4.0, 4.0)
    value_rows = jnp.clip(jax.random.normal(jax.random.fold_in(key, 12), shape, jnp.float32), -4.0, 4.0)
    return (key_rows, value_rows)


def draw_keyvals(key, part):
    key_rows, value_rows = shared_keys(key)
    stacked = jnp.stack([key_rows, value_rows], axis=2)
    return stacked.reshape(SECTIONS, 2, 2, SEQ, KVH * HD).astype(jnp.bfloat16)


def draw_queries(key, part):
    groups = HEADS // KVH
    shape = (SECTIONS, 2, SEQ, KVH, groups, HD)
    base = jnp.clip(2.5 * jax.random.normal(jax.random.fold_in(key, 13), shape, jnp.float32), -15.0, 15.0)
    return base.reshape(SECTIONS, 2, SEQ, HEADS * HD).astype(jnp.bfloat16)


def profile(amount, total, reach, lean):
    weights = [(1 << 20) // math.isqrt(standing ** lean) + 1 for standing in range(2, amount + 1)]
    surplus, holding = total - reach - (amount - 1), [1] * (amount - 1)
    while surplus > 0:
        movable = [i for i in range(amount - 1) if holding[i] < reach]
        pool, budget = sum([weights[i] for i in movable]), surplus
        for i in movable:
            extra = min(reach - holding[i], max(1, budget * weights[i] // pool), surplus)
            holding[i] = holding[i] + extra
            surplus = surplus - extra
    return np.array([reach] + holding)


def ragged_sizes(stream_key, number_of, total, limit, skew):
    if number_of == 2:
        one = jax.random.randint(stream_key, (), max(1, total - limit), min(limit, total - 1) + 1)
        return jnp.stack([one, total - one])
    sizes = jnp.asarray(profile(number_of, total, limit, skew), jnp.int32)
    couples = (number_of - 1) // 2
    giver, receiver = sizes[1:1 + 2 * couples:2], sizes[2:2 + 2 * couples:2]
    room = jnp.minimum(giver - 1, limit - receiver)
    moved = jax.random.randint(jax.random.fold_in(stream_key, 1), (couples,), 0, 1 << 20) % (room + 1)
    sizes = sizes.at[1:1 + 2 * couples:2].set(giver - moved).at[2:2 + 2 * couples:2].set(receiver + moved)
    return sizes[jax.random.permutation(jax.random.fold_in(stream_key, 2), number_of)]


def setup_inputs(seed: int = 0) -> dict:
    keys = jax.random.split(jax.random.key(seed), 4)
    queries = draw_queries(jax.random.fold_in(keys[3], 71), 0)
    keyvals = draw_keyvals(jax.random.fold_in(keys[3], 71), 0)
    segments = jax.vmap(lambda own: jnp.searchsorted(jnp.cumsum(ragged_sizes(own, 4, SEQ, 3 * SEQ // 4, 1)), jnp.arange(SEQ), side="right"))(jax.random.split(keys[2], SECTIONS * 2)).reshape((SECTIONS, 2, SEQ)).astype(jnp.int32)
    return dict(queries=queries, keyvals=keyvals, segments=segments)


def attend_stream(query_rows, key_value, doc_ids):
    groups = HEADS // KVH
    scale = 1.0 / math.sqrt(HD)
    query_heads = query_rows.reshape(SEQ, KVH, groups, HD).astype(jnp.float32)
    key_rows = key_value[0].reshape(SEQ, KVH, HD).astype(jnp.float32)
    value_rows = key_value[1].reshape(SEQ, KVH, HD).astype(jnp.float32)
    block_len = math.gcd(SEQ, 512)
    results = []
    for block_num in range(SEQ // block_len):
        first = block_num * block_len
        last_end = first + block_len
        query_block = query_heads[first:last_end]
        scores = jnp.einsum('tgjd,ngd->tgjn', query_block, key_rows[:last_end]) * scale
        query_pos = jnp.arange(first, last_end, dtype=jnp.int32)
        key_pos = jnp.arange(0, last_end, dtype=jnp.int32)
        allowed = (doc_ids[first:last_end, None] == doc_ids[None, :last_end]) & (key_pos[None, :] <= query_pos[:, None])
        allowed = allowed[:, None, None, :]
        scores = jnp.where(allowed, scores, -1e+30)
        row_max = lax.optimization_barrier(jnp.max(scores, axis=-1, keepdims=True))
        exp_terms = jnp.where(allowed, jnp.exp(scores - row_max), 0.0)
        row_sum = lax.optimization_barrier(jnp.sum(exp_terms, axis=-1))
        weights = lax.optimization_barrier(exp_terms.astype(jnp.bfloat16)).astype(jnp.float32)
        out_rows = jnp.einsum('tgjn,ngd->tgjd', weights, value_rows[:last_end]) / row_sum[..., None]
        results.append(out_rows.reshape(block_len, HEADS * HD).astype(jnp.bfloat16))
    return jnp.concatenate(results, axis=0)

def reference(queries, keyvals, segments):
    flat_queries = queries.reshape(SECTIONS * 2, SEQ, HEADS * HD)
    flat_keyvals = keyvals.reshape(SECTIONS * 2, 2, SEQ, KVH * HD)
    flat_segments = segments.reshape(SECTIONS * 2, SEQ)
    attended = lax.map(lambda entry_tuple: attend_stream(entry_tuple[0], entry_tuple[1], entry_tuple[2]), (flat_queries, flat_keyvals, flat_segments))
    attended = attended.reshape(SECTIONS, 2, SEQ, HEADS * HD)
    down_side = jnp.concatenate([attended[0:1, 1], attended[:-1, 0]], axis=0)
    up_side = jnp.concatenate([attended[1:, 1], attended[-1:, 0]], axis=0)
    return jnp.stack([down_side, up_side], axis=1)
```

```python
import functools
import math

import jax
import jax.numpy as jnp
from jax import lax
from jax.experimental import pallas as pl
from jax.experimental.pallas import tpu as pltpu
from jax.sharding import Mesh
from jax.sharding import PartitionSpec as P

HD = 128
KVH = 4
GROUPS = 8
ROWS = 8
YS = 4
PIECE = 64
CHUNK = 2 * PIECE + 16
BACK = 6
MASKED = -1e30


def attend_kernel(
    first, last, offsets, place, query_docs, queries, *refs
):
    count = len(offsets)
    messages = refs[:count]
    rest = refs[count:]
    if first:
        state_in = None
    else:
        state_in = rest[:3]
        rest = rest[3:]
    if last:
        (out_ref, max_ref, sum_ref, acc_ref) = rest
    else:
        (max_ref, sum_ref, acc_ref) = rest
    if state_in is not None:
        for source, target in zip(state_in, (max_ref, sum_ref, acc_ref)):
            target[...] = source[...]
    span = queries.shape[0]
    heads = queries.shape[1] // HD
    rate = math.log2(math.e) / math.sqrt(HD)
    docs = query_docs[0:1, :]
    first_doc = jnp.min(docs)
    last_doc = jnp.max(docs)
    row = place[0]

    def fold(message, offset, masked):
        diagonal = offset == 0
        keys = jnp.concatenate([message[c, :PIECE, :] for c in range(8)], axis=0)
        values = jnp.concatenate([message[c, PIECE : 2 * PIECE, :] for c in range(8)], axis=0)
        if masked:
            key_docs = message[:, 2 * PIECE, :].astype(jnp.float32)
            start = jnp.zeros((1, span), jnp.float32)
            for doc in range(1, 4):
                below = jnp.sum((key_docs < doc).astype(jnp.float32))
                start = jnp.where(docs == doc, below, start)
            start = start.astype(jnp.int32)
            key_pos = lax.broadcasted_iota(jnp.int32, (span, span), 0)
            allowed = key_pos >= start
            if diagonal:
                allowed = allowed & (key_pos <= lax.broadcasted_iota(jnp.int32, (span, span), 1))
        for head in range(heads):
            columns = slice(head * HD, (head + 1) * HD)
            scores = lax.dot_general(
                keys,
                queries[:, columns],
                (((1,), (1,)), ((), ())),
                preferred_element_type=jnp.float32,
            )
            if masked:
                scores = jnp.where(allowed, scores, MASKED)
            top = jnp.max(scores, axis=0, keepdims=True)
            if not diagonal:
                old_max = max_ref[head : head + 1, :]
                top = jnp.maximum(old_max, top)
            terms = jnp.exp2((scores - top) * rate)
            total = jnp.sum(terms, axis=0, keepdims=True)
            product = lax.dot_general(
                values,
                terms.astype(jnp.bfloat16),
                (((0,), (0,)), ((), ())),
                preferred_element_type=jnp.float32,
            )
            if not diagonal:
                factor = jnp.exp2((old_max - top) * rate)
                total = total + factor * sum_ref[head : head + 1, :]
                product = product + factor * acc_ref[head]
            max_ref[head : head + 1, :] = top
            sum_ref[head : head + 1, :] = total
            acc_ref[head] = product

    for message, offset in zip(messages, offsets):
        if offset == 0:
            fold(message, 0, True)
            continue

        @pl.when(row >= offset)
        def _(message=message, offset=offset):
            key_docs = message[:, 2 * PIECE, :PIECE].astype(jnp.float32)
            low = jnp.min(key_docs)
            high = jnp.max(key_docs)

            @pl.when(low == last_doc)
            def _():
                fold(message, offset, False)

            @pl.when((low < last_doc) & (high >= first_doc))
            def _():
                fold(message, offset, True)

    if last:
        for head in range(heads):
            columns = slice(head * HD, (head + 1) * HD)
            scaled = acc_ref[head] / sum_ref[head : head + 1, :]
            rows = jnp.transpose(scaled).astype(out_ref.dtype)
            for block in range(YS):
                slot = lax.rem(block + place[1], YS)
                out_ref[slot, :, columns] = rows[block * HD : (block + 1) * HD, :]


def attend(place, query_docs, queries, messages, offsets, state, last):
    span, width = queries.shape
    heads = width // HD
    state_shapes = [
        jax.ShapeDtypeStruct((heads, span), jnp.float32),
        jax.ShapeDtypeStruct((heads, span), jnp.float32),
        jax.ShapeDtypeStruct((heads, HD, span), jnp.float32),
    ]
    operands = [place, query_docs, queries, *messages]
    if state is not None:
        operands += list(state)
    vmem = pl.BlockSpec(memory_space=pltpu.VMEM)
    if last:
        out_shape = [jax.ShapeDtypeStruct((YS, span // YS, width), jnp.bfloat16)]
        scratch = [pltpu.VMEM(s.shape, s.dtype) for s in state_shapes]
    else:
        out_shape = state_shapes
        scratch = []
    keys = span * len(messages)
    return pl.pallas_call(
        functools.partial(attend_kernel, state is None, last, tuple(offsets)),
        out_shape=out_shape,
        in_specs=[pl.BlockSpec(memory_space=pltpu.SMEM)] + [vmem] * (len(operands) - 1),
        out_specs=[vmem] * len(out_shape),
        scratch_shapes=scratch,
        cost_estimate=pl.CostEstimate(
            flops=4 * heads * span * keys * HD,
            transcendentals=heads * span * keys,
            bytes_accessed=2 * span * width + 4 * heads * HD * span,
        ),
        compiler_params=pltpu.CompilerParams(vmem_limit_bytes=32 << 20),
        name="attend",
    )(*operands)


def local(queries, keyvals, segments):
    section = lax.axis_index("section")
    row = lax.axis_index("row")
    y = lax.axis_index("y")
    core = lax.axis_index("core")

    pieces = keyvals[0].reshape(2, 2, PIECE, KVH, HD).transpose(3, 0, 1, 2, 4)
    pieces = pieces.reshape(8, 2 * PIECE, HD)
    docs = segments[0].astype(jnp.bfloat16)
    docs = lax.dynamic_slice_in_dim(docs, core * PIECE, PIECE, 1)
    docs = jnp.pad(docs, ((0, 0), (0, HD - PIECE)), constant_values=9)
    docs = jnp.broadcast_to(docs[None, :, None, :], (KVH, 2, 16, HD)).reshape(8, 16, HD)
    message = jnp.concatenate([pieces, docs], axis=1)
    message = lax.all_to_all(message, ("y", "core"), 0, 0, tiled=True)

    messages = [message]
    for step in range(1, BACK + 1):
        route = [(a, a + 1) for a in range(step - 1, ROWS - 1)]
        messages.append(lax.ppermute(messages[-1], "row", route))

    own = lax.all_to_all(queries[0], "core", 0, 2, tiled=True)
    own = lax.all_to_all(own, "y", 2, 1, tiled=True)[0]

    query_docs = message[:, 2 * PIECE, :PIECE].reshape(1, 8 * PIECE).astype(jnp.float32)
    query_docs = jnp.broadcast_to(query_docs, (8, 8 * PIECE))
    goal = jnp.where(
        (section == 7) & (core == 0), 1, jnp.where((section == 0) & (core == 1), 0, core)
    )
    base = 2 * (y % 2) + goal
    place = jnp.stack([row, (YS - base) % YS]).astype(jnp.int32)

    state = None
    groups = [[0], [1], [2], [3], [4], [5], [6]]
    for group in groups:
        last = group is groups[-1]
        state = attend(
            place, query_docs, own, [messages[i] for i in group], group, state, last
        )
    out = state[0]

    received = []
    for turn in range(YS):
        route = []
        for s in range(8):
            for head in range(YS):
                for stream in range(2):
                    s_to = s + 1 - 2 * stream
                    slot = stream
                    if s_to < 0 or s_to > 7:
                        s_to, slot = s, 1 - stream
                    block = (2 * (head % 2) + slot + turn) % YS
                    route.append(((s * YS + head) * 2 + stream, (s_to * YS + block) * 2 + head // 2))
        received.append(lax.ppermute(out[turn], ("section", "y", "core"), route))
    stacked = jnp.stack(received)
    parts = [
        lax.dynamic_index_in_dim(stacked, (y - v) % YS, 0, keepdims=False) for v in range(YS)
    ]
    slots = [jnp.concatenate([parts[slot], parts[2 + slot]], axis=1) for slot in range(2)]
    return jnp.stack(slots)[None]


def solution(mesh):
    grid = Mesh(mesh.devices.reshape(8, ROWS, YS, 2), ("section", "row", "y", "core"))
    return jax.shard_map(
        local,
        mesh=grid,
        in_specs=(
            P("section", None, ("row", "y"), "core"),
            P("section", None, None, ("row", "y", "core"), None),
            P("section", None, ("row", "y")),
        ),
        out_specs=P("section", None, ("row", "y"), "core"),
        check_vma=False,
    )
```

```python
import functools
import math

import jax
import jax.numpy as jnp
from jax import lax
from jax.experimental import pallas as pl
from jax.experimental.pallas import tpu as pltpu
from jax.sharding import Mesh
from jax.sharding import PartitionSpec as P

HD = 128
KVH = 4
GROUPS = 8
ROWS = 8
YS = 4
PIECE = 64
CHUNK = 2 * PIECE + 16
BACK = 6
MASKED = -1e30


def attend_kernel(offset, last, place, query_docs, key_part, value_part, *refs):
    if offset:
        queries, *refs = refs
    if offset == 0:
        blocks, refs = refs[:YS], refs[YS:]
        (queries, max_ref, sum_ref, acc_ref, even, odd) = refs
        for turn, block in enumerate(blocks):
            home = lax.rem(place[2] + YS - turn, YS)
            queries[pl.ds(pl.multiple_of(home * HD, HD), HD), :] = block[...]
        old_max_ref = old_sum_ref = old_acc_ref = None
    elif last:
        (old_max_ref, old_sum_ref, old_acc_ref, _, out_ref) = refs[:5]
        (max_ref, sum_ref, acc_ref, even, odd) = refs[5:]
    else:
        (old_max_ref, old_sum_ref, old_acc_ref) = refs[:3]
        (max_ref, sum_ref, acc_ref, even, odd) = refs[3:]
    span = queries.shape[0]
    heads = queries.shape[1] // HD
    rate = math.log2(math.e) / math.sqrt(HD)
    docs = query_docs[0:1, :]

    def fold(masked):
        keys = key_part[:span, :]
        values = value_part[...]
        if masked:
            key_docs = key_part[span : span + YS, :].astype(jnp.float32)
            start = jnp.zeros((1, span), jnp.float32)
            for doc in range(1, 4):
                below = jnp.sum((key_docs < doc).astype(jnp.float32))
                start = jnp.where(docs == doc, below, start)
            start = start.astype(jnp.int32)

        def score(head):
            columns = pl.ds(pl.multiple_of(head * HD, HD), HD)
            return lax.dot_general(
                keys,
                queries[:, columns],
                (((1,), (1,)), ((), ())),
                preferred_element_type=jnp.float32,
            )

        def one_head(head, scores):
            if masked:
                key_pos = lax.broadcasted_iota(jnp.int32, (span, span), 0)
                allowed = key_pos >= start
                if offset == 0:
                    query_pos = lax.broadcasted_iota(jnp.int32, (span, span), 1)
                    allowed = allowed & (key_pos <= query_pos)
                scores = jnp.where(allowed, scores, MASKED)
            top = jnp.max(scores, axis=0, keepdims=True)
            if offset:
                old_max = old_max_ref[pl.ds(head, 1), :]
                top = jnp.maximum(old_max, top)
            terms = jnp.exp2((scores - top) * rate)
            total = jnp.sum(terms, axis=0, keepdims=True)
            product = lax.dot_general(
                values,
                terms.astype(jnp.bfloat16),
                (((0,), (0,)), ((), ())),
                preferred_element_type=jnp.float32,
            )
            if offset:
                factor = jnp.exp2((old_max - top) * rate)
                total = total + factor * old_sum_ref[pl.ds(head, 1), :]
                product = product + factor * old_acc_ref[head]
            max_ref[pl.ds(head, 1), :] = top
            sum_ref[pl.ds(head, 1), :] = total
            acc_ref[head] = product

        def two_heads(pair, _):
            odd[...] = score(2 * pair + 1)
            one_head(2 * pair, even[...])
            even[...] = score(jnp.minimum(2 * pair + 2, heads - 1))
            one_head(2 * pair + 1, odd[...])
            return 0

        even[...] = score(0)
        lax.fori_loop(0, heads // 2, two_heads, 0)

    if offset == 0:
        fold(True)
    else:
        key_docs = key_part[span : span + YS, :].astype(jnp.float32)
        low = jnp.min(key_docs)
        first_doc = jnp.min(docs)
        last_doc = jnp.max(docs)
        live = (place[0] >= offset) & (jnp.max(key_docs) >= first_doc)
        pl.when(live & (low >= last_doc))(functools.partial(fold, False))
        pl.when(live & (low < last_doc))(functools.partial(fold, True))

        @pl.when(jnp.logical_not(live))
        def _():
            for source, target in zip(
                (old_max_ref, old_sum_ref, old_acc_ref), (max_ref, sum_ref, acc_ref)
            ):
                target[...] = source[...]

    if last:

        def one_result(head, _):
            columns = pl.ds(pl.multiple_of(head * HD, HD), HD)
            scaled = acc_ref[head] / sum_ref[pl.ds(head, 1), :]
            rows = jnp.transpose(scaled).astype(out_ref.dtype)
            for block in range(YS):
                slot = lax.rem(block + place[1], YS)
                out_ref[slot, :, columns] = rows[block * HD : (block + 1) * HD, :]
            return 0

        lax.fori_loop(0, heads, one_result, 0)


def attend(place, query_docs, parts, offset, held, last):
    span = YS * HD
    width = GROUPS * HD
    state_shapes = [
        jax.ShapeDtypeStruct((GROUPS, span), jnp.float32),
        jax.ShapeDtypeStruct((GROUPS, span), jnp.float32),
        jax.ShapeDtypeStruct((GROUPS, HD, span), jnp.float32),
    ]
    operands = [place, query_docs, *parts, *held]
    vmem = pl.BlockSpec(memory_space=pltpu.VMEM)
    scratch = [pltpu.VMEM((span, span), jnp.float32)] * 2
    out_shape = state_shapes
    if last:
        out_shape = [jax.ShapeDtypeStruct((YS, span // YS, width), jnp.bfloat16)]
        scratch = [pltpu.VMEM(s.shape, s.dtype) for s in state_shapes] + scratch
    elif offset == 0:
        out_shape = [jax.ShapeDtypeStruct((span, width), jnp.bfloat16)] + state_shapes
    return pl.pallas_call(
        functools.partial(attend_kernel, offset, last),
        out_shape=out_shape,
        in_specs=[pl.BlockSpec(memory_space=pltpu.SMEM)] + [vmem] * (len(operands) - 1),
        out_specs=[vmem] * len(out_shape),
        scratch_shapes=scratch,
        cost_estimate=pl.CostEstimate(
            flops=4 * GROUPS * span * span * HD,
            transcendentals=GROUPS * span * span,
            bytes_accessed=2 * span * width + 8 * GROUPS * HD * span,
        ),
        compiler_params=pltpu.CompilerParams(vmem_limit_bytes=32 << 20),
        name="attend",
    )(*operands)


def local(queries, keyvals, segments):
    section = lax.axis_index("section")
    row = lax.axis_index("row")
    y = lax.axis_index("y")
    core = lax.axis_index("core")

    source = queries[0]
    blocks = []
    for turn in range(YS):
        route = []
        for a in range(YS):
            for half in range(2):
                job = (a + turn) % YS
                route.append((2 * a + half, 2 * (2 * half + job // 2) + job % 2))
        job = (y + turn) % YS
        block = lax.dynamic_slice(
            source, (job % 2, 0, (job // 2) * GROUPS * HD), (1, HD, GROUPS * HD)
        )
        blocks.append(lax.ppermute(block[0], ("y", "core"), route))

    pieces = keyvals[0].reshape(2, 2, PIECE, KVH, HD).transpose(3, 0, 1, 2, 4)
    pieces = pieces.reshape(8, 2 * PIECE, HD)
    docs = segments[0].astype(jnp.bfloat16)
    docs = lax.dynamic_slice_in_dim(docs, core * PIECE, PIECE, 1)
    docs = jnp.pad(docs, ((0, 0), (0, HD - PIECE)), constant_values=9)
    docs = jnp.broadcast_to(docs[None, :, None, :], (KVH, 2, 16, HD)).reshape(8, 16, HD)
    message = jnp.concatenate([pieces, docs], axis=1)
    message = lax.all_to_all(message, ("y", "core"), 0, 0, tiled=True)

    docs = message[:, 2 * PIECE, :PIECE].reshape(YS, HD)
    key_part = jnp.concatenate(
        [message[:, :PIECE].reshape(YS * HD, HD), jnp.pad(docs, ((0, 16 - YS), (0, 0)))]
    )
    value_part = message[:, PIECE : 2 * PIECE].reshape(YS * HD, HD)
    query_docs = jnp.broadcast_to(docs.reshape(1, YS * HD).astype(jnp.float32), (8, YS * HD))
    goal = jnp.where(
        (section == 7) & (core == 0), 1, jnp.where((section == 0) & (core == 1), 0, core)
    )
    base = 2 * (y % 2) + goal
    place = jnp.stack([row, (YS - base) % YS, 2 * (y % 2) + core]).astype(jnp.int32)

    def hop(part, step):
        route = [(a, a + 1) for a in range(step - 1, ROWS - 1)]
        return tuple(lax.ppermute(x, "row", route) for x in part)

    own_part = (key_part, value_part)
    part = hop(own_part, 1)
    own, *state = attend(place, query_docs, own_part, 0, blocks, False)
    token = None
    for step in range(1, BACK + 1):
        if step < BACK:
            keys, state = lax.optimization_barrier((part[0], state))
            part = (keys, part[1])
            later = hop(part, step + 1)
        if step == BACK - 1:
            token = lax.ppermute(part[0][YS * HD :], "row", [(7, 3), (6, 2), (5, 4)])
            token = token + lax.ppermute(token, "row", [(3, 1), (2, 0)])
        held = [own, *state] + ([token] if step == BACK else [])
        state = attend(place, query_docs, part, step, held, step == BACK)
        part = later
    out = state[0]

    received = []
    for turn in range(YS):
        route = []
        for s in range(8):
            for head in range(YS):
                for stream in range(2):
                    s_to = s + 1 - 2 * stream
                    slot = stream
                    if s_to < 0 or s_to > 7:
                        s_to, slot = s, 1 - stream
                    block = (2 * (head % 2) + slot + turn) % YS
                    route.append(((s * YS + head) * 2 + stream, (s_to * YS + block) * 2 + head // 2))
        received.append(lax.ppermute(out[turn], ("section", "y", "core"), route))
    stacked = jnp.stack(received)
    parts = [
        lax.dynamic_index_in_dim(stacked, (y - v) % YS, 0, keepdims=False) for v in range(YS)
    ]
    slots = [jnp.concatenate([parts[slot], parts[2 + slot]], axis=1) for slot in range(2)]
    return jnp.stack(slots)[None]


def solution(mesh):
    grid = Mesh(mesh.devices.reshape(8, ROWS, YS, 2), ("section", "row", "y", "core"))
    return jax.shard_map(
        local,
        mesh=grid,
        in_specs=(
            P("section", None, ("row", "y"), "core"),
            P("section", None, None, ("row", "y", "core"), None),
            P("section", None, ("row", "y")),
        ),
        out_specs=P("section", None, ("row", "y"), "core"),
        check_vma=False,
    )
```

```python
import functools
import math

import jax
import jax.numpy as jnp
from jax import lax
from jax.experimental import pallas as pl
from jax.experimental.pallas import tpu as pltpu
from jax.sharding import Mesh
from jax.sharding import PartitionSpec as P

HD = 128
KVH = 4
GROUPS = 8
ROWS = 8
YS = 4
PIECE = 64
CHUNK = 2 * PIECE + 16
BACK = 6
MASKED = -1e30


def attend_kernel(offset, last, place, query_docs, key_part, value_part, *refs):
    if offset:
        queries, *refs = refs
    if offset == 0:
        blocks, refs = refs[:YS], refs[YS:]
        (queries, max_ref, sum_ref, acc_ref, even, odd) = refs
        for turn, block in enumerate(blocks):
            home = lax.rem(place[2] + YS - turn, YS)
            queries[pl.ds(pl.multiple_of(home * HD, HD), HD), :] = block[...]
        old_max_ref = old_sum_ref = old_acc_ref = None
    elif last:
        (old_max_ref, old_sum_ref, old_acc_ref, _, out_ref) = refs[:5]
        (max_ref, sum_ref, acc_ref, even, odd) = refs[5:]
    else:
        (old_max_ref, old_sum_ref, old_acc_ref) = refs[:3]
        (max_ref, sum_ref, acc_ref, even, odd) = refs[3:]
    span = queries.shape[0]
    heads = queries.shape[1] // HD
    rate = math.log2(math.e) / math.sqrt(HD)
    docs = query_docs[0:1, :]

    key_docs = key_part[span : span + YS, :].astype(jnp.float32)

    def fold(single):
        keys = key_part[:span, :]
        values = value_part[...]
        if single:
            whole = docs == jnp.max(key_docs)
        else:
            start = jnp.zeros((1, span), jnp.float32)
            for doc in range(1, 4):
                below = jnp.sum((key_docs < doc).astype(jnp.float32))
                start = jnp.where(docs == doc, below, start)
            start = start.astype(jnp.int32)

        def score(head):
            columns = pl.ds(pl.multiple_of(head * HD, HD), HD)
            return lax.dot_general(
                keys,
                queries[:, columns],
                (((1,), (1,)), ((), ())),
                preferred_element_type=jnp.float32,
            )

        def one_head(head, scores):
            if not single:
                key_pos = lax.broadcasted_iota(jnp.int32, (span, span), 0)
                allowed = key_pos >= start
                if offset == 0:
                    query_pos = lax.broadcasted_iota(jnp.int32, (span, span), 1)
                    allowed = allowed & (key_pos <= query_pos)
                scores = jnp.where(allowed, scores, MASKED)
            top = jnp.max(scores, axis=0, keepdims=True)
            if offset:
                old_max = old_max_ref[pl.ds(head, 1), :]
                top = jnp.maximum(old_max, top)
            shift = top
            if single:
                top = jnp.where(whole, top, old_max)
                shift = jnp.where(whole, top, -MASKED)
            terms = jnp.exp2((scores - shift) * rate)
            total = jnp.sum(terms, axis=0, keepdims=True)
            product = lax.dot_general(
                values,
                terms.astype(jnp.bfloat16),
                (((0,), (0,)), ((), ())),
                preferred_element_type=jnp.float32,
            )
            if offset:
                factor = jnp.exp2((old_max - top) * rate)
                total = total + factor * old_sum_ref[pl.ds(head, 1), :]
                product = product + factor * old_acc_ref[head]
            max_ref[pl.ds(head, 1), :] = top
            sum_ref[pl.ds(head, 1), :] = total
            acc_ref[head] = product

        def two_heads(pair, _):
            odd[...] = score(2 * pair + 1)
            one_head(2 * pair, even[...])
            even[...] = score(jnp.minimum(2 * pair + 2, heads - 1))
            one_head(2 * pair + 1, odd[...])
            return 0

        even[...] = score(0)
        lax.fori_loop(0, heads // 2, two_heads, 0)

    if offset == 0:
        fold(False)
    else:
        low = jnp.min(key_docs)
        high = jnp.max(key_docs)
        live = (place[0] >= offset) & (high >= jnp.min(docs))
        pl.when(live & (low == high))(functools.partial(fold, True))
        pl.when(live & (low < high))(functools.partial(fold, False))

        @pl.when(jnp.logical_not(live))
        def _():
            for source, target in zip(
                (old_max_ref, old_sum_ref, old_acc_ref), (max_ref, sum_ref, acc_ref)
            ):
                target[...] = source[...]

    if last:

        def one_result(head, _):
            columns = pl.ds(pl.multiple_of(head * HD, HD), HD)
            scaled = acc_ref[head] / sum_ref[pl.ds(head, 1), :]
            rows = jnp.transpose(scaled).astype(out_ref.dtype)
            for block in range(YS):
                slot = lax.rem(block + place[1], YS)
                out_ref[slot, :, columns] = rows[block * HD : (block + 1) * HD, :]
            return 0

        lax.fori_loop(0, heads, one_result, 0)


def attend(place, query_docs, parts, offset, held, last):
    span = YS * HD
    width = GROUPS * HD
    state_shapes = [
        jax.ShapeDtypeStruct((GROUPS, span), jnp.float32),
        jax.ShapeDtypeStruct((GROUPS, span), jnp.float32),
        jax.ShapeDtypeStruct((GROUPS, HD, span), jnp.float32),
    ]
    operands = [place, query_docs, *parts, *held]
    vmem = pl.BlockSpec(memory_space=pltpu.VMEM)
    scratch = [pltpu.VMEM((span, span), jnp.float32)] * 2
    out_shape = state_shapes
    if last:
        out_shape = [jax.ShapeDtypeStruct((YS, span // YS, width), jnp.bfloat16)]
        scratch = [pltpu.VMEM(s.shape, s.dtype) for s in state_shapes] + scratch
    elif offset == 0:
        out_shape = [jax.ShapeDtypeStruct((span, width), jnp.bfloat16)] + state_shapes
    return pl.pallas_call(
        functools.partial(attend_kernel, offset, last),
        out_shape=out_shape,
        in_specs=[pl.BlockSpec(memory_space=pltpu.SMEM)] + [vmem] * (len(operands) - 1),
        out_specs=[vmem] * len(out_shape),
        scratch_shapes=scratch,
        cost_estimate=pl.CostEstimate(
            flops=4 * GROUPS * span * span * HD,
            transcendentals=GROUPS * span * span,
            bytes_accessed=2 * span * width + 8 * GROUPS * HD * span,
        ),
        compiler_params=pltpu.CompilerParams(vmem_limit_bytes=32 << 20),
        name="attend",
    )(*operands)


def local(queries, keyvals, segments):
    section = lax.axis_index("section")
    row = lax.axis_index("row")
    y = lax.axis_index("y")
    core = lax.axis_index("core")

    source = queries[0]
    blocks = []
    for turn in range(YS):
        route = []
        for a in range(YS):
            for half in range(2):
                job = (a + turn) % YS
                route.append((2 * a + half, 2 * (2 * half + job // 2) + job % 2))
        job = (y + turn) % YS
        block = lax.dynamic_slice(
            source, (job % 2, 0, (job // 2) * GROUPS * HD), (1, HD, GROUPS * HD)
        )
        blocks.append(lax.ppermute(block[0], ("y", "core"), route))

    pieces = keyvals[0].reshape(2, 2, PIECE, KVH, HD).transpose(3, 0, 1, 2, 4)
    pieces = pieces.reshape(8, 2 * PIECE, HD)
    docs = segments[0].astype(jnp.bfloat16)
    docs = lax.dynamic_slice_in_dim(docs, core * PIECE, PIECE, 1)
    docs = jnp.pad(docs, ((0, 0), (0, HD - PIECE)), constant_values=9)
    docs = jnp.broadcast_to(docs[None, :, None, :], (KVH, 2, 16, HD)).reshape(8, 16, HD)
    message = jnp.concatenate([pieces, docs], axis=1)
    message = lax.all_to_all(message, ("y", "core"), 0, 0, tiled=True)

    docs = message[:, 2 * PIECE, :PIECE].reshape(YS, HD)
    key_part = jnp.concatenate(
        [message[:, :PIECE].reshape(YS * HD, HD), jnp.pad(docs, ((0, 16 - YS), (0, 0)))]
    )
    value_part = message[:, PIECE : 2 * PIECE].reshape(YS * HD, HD)
    query_docs = jnp.broadcast_to(docs.reshape(1, YS * HD).astype(jnp.float32), (8, YS * HD))
    goal = jnp.where(
        (section == 7) & (core == 0), 1, jnp.where((section == 0) & (core == 1), 0, core)
    )
    base = 2 * (y % 2) + goal
    place = jnp.stack([row, (YS - base) % YS, 2 * (y % 2) + core]).astype(jnp.int32)

    def hop(part, step):
        route = [(a, a + 1) for a in range(step - 1, ROWS - 1)]
        return tuple(lax.ppermute(x, "row", route) for x in part)

    own_part = (key_part, value_part)
    part = hop(own_part, 1)
    own, *state = attend(place, query_docs, own_part, 0, blocks, False)
    token = None
    for step in range(1, BACK + 1):
        if step < BACK:
            keys, state = lax.optimization_barrier((part[0], state))
            part = (keys, part[1])
            later = hop(part, step + 1)
        if step == BACK - 1:
            token = lax.ppermute(part[0][YS * HD :], "row", [(7, 3), (6, 2)])
        held = [own, *state] + ([token] if step == BACK else [])
        state = attend(place, query_docs, part, step, held, step == BACK)
        part = later
    out = state[0]

    received = []
    for turn in range(YS):
        route = []
        for s in range(8):
            for head in range(YS):
                for stream in range(2):
                    s_to = s + 1 - 2 * stream
                    slot = stream
                    if s_to < 0 or s_to > 7:
                        s_to, slot = s, 1 - stream
                    block = (2 * (head % 2) + slot + turn) % YS
                    route.append(((s * YS + head) * 2 + stream, (s_to * YS + block) * 2 + head // 2))
        received.append(lax.ppermute(out[turn], ("section", "y", "core"), route))
    stacked = jnp.stack(received)
    parts = [
        lax.dynamic_index_in_dim(stacked, (y - v) % YS, 0, keepdims=False) for v in range(YS)
    ]
    slots = [jnp.concatenate([parts[slot], parts[2 + slot]], axis=1) for slot in range(2)]
    return jnp.stack(slots)[None]


def solution(mesh):
    grid = Mesh(mesh.devices.reshape(8, ROWS, YS, 2), ("section", "row", "y", "core"))
    return jax.shard_map(
        local,
        mesh=grid,
        in_specs=(
            P("section", None, ("row", "y"), "core"),
            P("section", None, None, ("row", "y", "core"), None),
            P("section", None, ("row", "y")),
        ),
        out_specs=P("section", None, ("row", "y"), "core"),
        check_vma=False,
    )
```

```python
import functools
import math

import jax
import jax.numpy as jnp
from jax import lax
from jax.experimental import pallas as pl
from jax.experimental.pallas import tpu as pltpu
from jax.sharding import Mesh
from jax.sharding import PartitionSpec as P

HD = 128
KVH = 4
GROUPS = 8
ROWS = 8
YS = 4
PIECE = 64
CHUNK = 2 * PIECE + 16
BACK = 6
MASKED = -1e30


def attend_kernel(offset, last, place, query_docs, key_part, value_part, *refs):
    if offset:
        queries, *refs = refs
    if offset == 0:
        blocks, refs = refs[:YS], refs[YS:]
        (queries, max_ref, sum_ref, acc_ref, even, odd) = refs
        for turn, block in enumerate(blocks):
            home = lax.rem(place[2] + YS - turn, YS)
            queries[pl.ds(pl.multiple_of(home * HD, HD), HD), :] = block[...]
        old_max_ref = old_sum_ref = old_acc_ref = None
    elif last:
        (old_max_ref, old_sum_ref, old_acc_ref, _, out_ref) = refs[:5]
        (max_ref, sum_ref, acc_ref, even, odd) = refs[5:]
    else:
        (old_max_ref, old_sum_ref, old_acc_ref) = refs[:3]
        (max_ref, sum_ref, acc_ref, even, odd) = refs[3:]
    span = queries.shape[0]
    heads = queries.shape[1] // HD
    rate = math.log2(math.e) / math.sqrt(HD)
    docs = query_docs[0:1, :]

    key_docs = key_part[span : span + YS, :].astype(jnp.float32)

    def fold(single):
        keys = key_part[:span, :]
        values = value_part[...]
        if single:
            whole = docs == jnp.max(key_docs)
        else:
            start = jnp.zeros((1, span), jnp.float32)
            for doc in range(1, 4):
                below = jnp.sum((key_docs < doc).astype(jnp.float32))
                start = jnp.where(docs == doc, below, start)
            start = start.astype(jnp.int32)

        def score(head):
            columns = pl.ds(pl.multiple_of(head * HD, HD), HD)
            return lax.dot_general(
                keys,
                queries[:, columns],
                (((1,), (1,)), ((), ())),
                preferred_element_type=jnp.float32,
            )

        def one_head(head, scores):
            if not single:
                key_pos = lax.broadcasted_iota(jnp.int32, (span, span), 0)
                allowed = key_pos >= start
                if offset == 0:
                    query_pos = lax.broadcasted_iota(jnp.int32, (span, span), 1)
                    allowed = allowed & (key_pos <= query_pos)
                scores = jnp.where(allowed, scores, MASKED)
            top = jnp.max(scores, axis=0, keepdims=True)
            if offset:
                old_max = old_max_ref[pl.ds(head, 1), :]
                top = jnp.maximum(old_max, top)
            shift = top
            if single:
                top = jnp.where(whole, top, old_max)
                shift = jnp.where(whole, top, -MASKED)
            terms = jnp.exp2((scores - shift) * rate)
            total = jnp.sum(terms, axis=0, keepdims=True)
            product = lax.dot_general(
                values,
                terms.astype(jnp.bfloat16),
                (((0,), (0,)), ((), ())),
                preferred_element_type=jnp.float32,
            )
            if offset:
                factor = jnp.exp2((old_max - top) * rate)
                total = total + factor * old_sum_ref[pl.ds(head, 1), :]
                product = product + factor * old_acc_ref[head]
            max_ref[pl.ds(head, 1), :] = top
            sum_ref[pl.ds(head, 1), :] = total
            acc_ref[head] = product

        def two_heads(pair, _):
            odd[...] = score(2 * pair + 1)
            one_head(2 * pair, even[...])
            even[...] = score(jnp.minimum(2 * pair + 2, heads - 1))
            one_head(2 * pair + 1, odd[...])
            return 0

        even[...] = score(0)
        lax.fori_loop(0, heads // 2, two_heads, 0)

    if offset == 0:
        fold(False)
    else:
        low = jnp.min(key_docs)
        high = jnp.max(key_docs)
        live = (place[0] >= offset) & (high >= jnp.min(docs))
        pl.when(live & (low == high))(functools.partial(fold, True))
        pl.when(live & (low < high))(functools.partial(fold, False))

        @pl.when(jnp.logical_not(live))
        def _():
            for source, target in zip(
                (old_max_ref, old_sum_ref, old_acc_ref), (max_ref, sum_ref, acc_ref)
            ):
                target[...] = source[...]

    if last:

        def one_result(head, _):
            columns = pl.ds(pl.multiple_of(head * HD, HD), HD)
            scaled = acc_ref[head] / sum_ref[pl.ds(head, 1), :]
            rows = jnp.transpose(scaled).astype(out_ref.dtype)
            for block in range(YS):
                slot = lax.rem(block + place[1], YS)
                out_ref[slot, :, columns] = rows[block * HD : (block + 1) * HD, :]
            return 0

        lax.fori_loop(0, heads, one_result, 0)


def attend(place, query_docs, parts, offset, held, last):
    span = YS * HD
    width = GROUPS * HD
    state_shapes = [
        jax.ShapeDtypeStruct((GROUPS, span), jnp.float32),
        jax.ShapeDtypeStruct((GROUPS, span), jnp.float32),
        jax.ShapeDtypeStruct((GROUPS, HD, span), jnp.float32),
    ]
    operands = [place, query_docs, *parts, *held]
    vmem = pl.BlockSpec(memory_space=pltpu.VMEM)
    scratch = [pltpu.VMEM((span, span), jnp.float32)] * 2
    out_shape = state_shapes
    if last:
        out_shape = [jax.ShapeDtypeStruct((YS, span // YS, width), jnp.bfloat16)]
        scratch = [pltpu.VMEM(s.shape, s.dtype) for s in state_shapes] + scratch
    elif offset == 0:
        out_shape = [jax.ShapeDtypeStruct((span, width), jnp.bfloat16)] + state_shapes
    return pl.pallas_call(
        functools.partial(attend_kernel, offset, last),
        out_shape=out_shape,
        in_specs=[pl.BlockSpec(memory_space=pltpu.SMEM)] + [vmem] * (len(operands) - 1),
        out_specs=[vmem] * len(out_shape),
        scratch_shapes=scratch,
        cost_estimate=pl.CostEstimate(
            flops=4 * GROUPS * span * span * HD,
            transcendentals=GROUPS * span * span,
            bytes_accessed=2 * span * width + 8 * GROUPS * HD * span,
        ),
        compiler_params=pltpu.CompilerParams(vmem_limit_bytes=32 << 20),
        name="attend",
    )(*operands)


def local(queries, keyvals, segments):
    section = lax.axis_index("section")
    row = lax.axis_index("row")
    y = lax.axis_index("y")
    core = lax.axis_index("core")

    source = queries[0]
    blocks = []
    for turn in range(YS):
        route = []
        for a in range(YS):
            for half in range(2):
                job = (a + turn) % YS
                route.append((2 * a + half, 2 * (2 * half + job // 2) + job % 2))
        job = (y + turn) % YS
        block = lax.dynamic_slice(
            source, (job % 2, 0, (job // 2) * GROUPS * HD), (1, HD, GROUPS * HD)
        )
        blocks.append(lax.ppermute(block[0], ("y", "core"), route))

    pieces = keyvals[0].reshape(2, 2, PIECE, KVH, HD).transpose(3, 0, 1, 2, 4)
    pieces = pieces.reshape(8, 2 * PIECE, HD)
    docs = segments[0].astype(jnp.bfloat16)
    docs = lax.dynamic_slice_in_dim(docs, core * PIECE, PIECE, 1)
    docs = jnp.pad(docs, ((0, 0), (0, HD - PIECE)), constant_values=9)
    docs = jnp.broadcast_to(docs[None, :, None, :], (KVH, 2, 16, HD)).reshape(8, 16, HD)
    message = jnp.concatenate([pieces, docs], axis=1)
    message = lax.all_to_all(message, ("y", "core"), 0, 0, tiled=True)

    docs = message[:, 2 * PIECE, :PIECE].reshape(YS, HD)
    key_part = jnp.concatenate(
        [message[:, :PIECE].reshape(YS * HD, HD), jnp.pad(docs, ((0, 16 - YS), (0, 0)))]
    )
    value_part = message[:, PIECE : 2 * PIECE].reshape(YS * HD, HD)
    query_docs = jnp.broadcast_to(docs.reshape(1, YS * HD).astype(jnp.float32), (8, YS * HD))
    goal = jnp.where(
        (section == 7) & (core == 0), 1, jnp.where((section == 0) & (core == 1), 0, core)
    )
    base = 2 * (y % 2) + goal
    place = jnp.stack([row, (YS - base) % YS, 2 * (y % 2) + core]).astype(jnp.int32)

    def hop(part, step):
        route = [(a, a + 1) for a in range(step - 1, ROWS - 1)]
        return tuple(lax.ppermute(x, "row", route) for x in part)

    own_part = (key_part, value_part)
    part = hop(own_part, 1)
    own, *state = attend(place, query_docs, own_part, 0, blocks, False)
    token = None
    for step in range(1, BACK + 1):
        if step < BACK:
            keys, state = lax.optimization_barrier((part[0], state))
            part = (keys, part[1])
            later = hop(part, step + 1)
        if step == BACK - 2:
            token = lax.ppermute(part[0][YS * HD :], "row", [(7, 3), (6, 2), (5, 4)])
        held = [own, *state] + ([token] if step == BACK else [])
        state = attend(place, query_docs, part, step, held, step == BACK)
        part = later
    out = state[0]

    received = []
    for turn in range(YS):
        route = []
        for s in range(8):
            for head in range(YS):
                for stream in range(2):
                    s_to = s + 1 - 2 * stream
                    slot = stream
                    if s_to < 0 or s_to > 7:
                        s_to, slot = s, 1 - stream
                    block = (2 * (head % 2) + slot + turn) % YS
                    route.append(((s * YS + head) * 2 + stream, (s_to * YS + block) * 2 + head // 2))
        received.append(lax.ppermute(out[turn], ("section", "y", "core"), route))
    stacked = jnp.stack(received)
    parts = [
        lax.dynamic_index_in_dim(stacked, (y - v) % YS, 0, keepdims=False) for v in range(YS)
    ]
    slots = [jnp.concatenate([parts[slot], parts[2 + slot]], axis=1) for slot in range(2)]
    return jnp.stack(slots)[None]


def solution(mesh):
    grid = Mesh(mesh.devices.reshape(8, ROWS, YS, 2), ("section", "row", "y", "core"))
    return jax.shard_map(
        local,
        mesh=grid,
        in_specs=(
            P("section", None, ("row", "y"), "core"),
            P("section", None, None, ("row", "y", "core"), None),
            P("section", None, ("row", "y")),
        ),
        out_specs=P("section", None, ("row", "y"), "core"),
        check_vma=False,
    )
```
